32 devices in a mesh: blk: 8 (over z, core), fiber: 4 (over y, x).
Axes of the slice: x: 2, y: 2, z: 4, core: 2. Of those that a mesh axis runs over, the one named last changes fastest.
Arguments:
- embedding: bfloat16 [16384, 256], P(('blk', 'fiber')), may hold values from -2.09375 to 2.09375
- tile_dest: int32 [8, 4, 8, 24], P('blk', 'fiber'), may hold values from 0 to 15, as said below
- tile_source: int32 [8, 4, 8, 24], P('blk', 'fiber'), may hold values from 0 to 3
- tile_count: int32 [8, 4, 8], P('blk', 'fiber'), may hold values from 2 to 24, as said below
- pattern_id: int32 [8, 4, 8, 24], P('blk', 'fiber'), may hold values from 0 to 63
- pattern_bank: int32 [64, 4, 128], replicated, may hold values from -2147483648 to 2147483646
- negative_dest: int32 [8, 4, 8, 4], P('blk', 'fiber'), may hold values from 0 to 15
- negative_source: int32 [8, 4, 8, 4], P('blk', 'fiber'), may hold values from 0 to 3
Outputs:
- gradient: float32 [16384, 256], P(('blk', 'fiber'))
The draws below stay inside these ranges and needn't reach their ends.
Inputs may be any that keep to these rules, and one draw needn't show every extreme that they name: At each block, fiber and stop the 24 pairs (tile_dest, tile_source) are distinct. `tile_count`: slots at or past the count are unused; some block, fiber and stop lists 24 tiles.
All inputs are finite; a program needn't handle non-finite values.
Results may differ from the reference program's by a relative error of at most 0.00064.
Values may be sent and summed in bfloat16 or wider, within the bound.
No kernel may reach another device: no remote copies, remote signals or barrier semaphores. Data moves between devices by JAX's collectives and lax.ppermute only.
A program may use at most 64 MiB of HBM per device.

```python
import jax
import jax.numpy as jnp
from jax import lax

D = 256
TILE = 128
SUB = 4
CAP = 24
NEG = 4
BANK = 64
WORDS = 4
STOPS = 8
FIBERS = 4
PT = 16
NODES = 16384


def shuffled_pairs(base_key):
    key_list = jax.random.split(jax.random.fold_in(base_key, 11), STOPS * FIBERS * STOPS)

    def first_pairs(one_key):
        return jax.random.permutation(one_key, PT * SUB)[:CAP]
    pair_ids = jax.vmap(first_pairs)(key_list)
    return pair_ids.reshape(STOPS, FIBERS, STOPS, CAP).astype(jnp.int32)


def draw_tile_dest(key, part):
    return (shuffled_pairs(key) // SUB).astype(jnp.int32)


def draw_tile_source(key, part):
    return (shuffled_pairs(key) % SUB).astype(jnp.int32)


def draw_tile_count(key, part):
    first_key, second_key = jax.random.split(jax.random.fold_in(key, 5))
    device_level = jax.random.randint(first_key, (STOPS, FIBERS, 1), 2, 5)
    base_count = jax.random.randint(second_key, (STOPS, FIBERS, STOPS), 2, CAP // 2 + 2)
    listed_count = jnp.minimum(base_count * device_level // 2, CAP)
    return listed_count.at[0, 0, 0].set(CAP).astype(jnp.int32)


def with_ends(entries, key, smallest, largest):
    dims = entries.shape
    spot = [jax.random.randint(jax.random.fold_in(key, axis), (), 0, dims[axis]) for axis in range(len(dims))]
    entries = entries.at[tuple(spot)].set(smallest)
    longest = dims.index(max(dims))
    spot[longest] = (spot[longest] + 1) % dims[longest]
    return entries.at[tuple(spot)].set(largest)


def levels(key, dims, cuts, least, largest):
    def one(axis_at, shards_of):
        steps = jax.random.uniform(jax.random.fold_in(jax.random.fold_in(key, 6), axis_at), (shards_of,), jnp.float32, least / len(cuts), largest / len(cuts))
        return jnp.repeat(jnp.exp(steps), dims[axis_at] // shards_of).reshape((-1,) + (1,) * (len(dims) - axis_at - 1))

    gain = one(*cuts[0])
    for cut in cuts[1:]:
        gain = gain * one(*cut)
    return gain


def scatter_about(rng, extent, deviation, most, cuts=(), kind=jnp.bfloat16):
    factor_of = levels(rng, extent, cuts, -0.22, 0.18) if cuts else 1.0
    entries = jax.random.normal(rng, extent, jnp.float32) * deviation * factor_of
    return jnp.minimum(jnp.maximum(entries, -most), most).astype(kind)


def setup_inputs(seed: int = 0) -> dict:
    arg_keys = jax.random.split(jax.random.key(seed), 9)
    return {
        "embedding": scatter_about(arg_keys[0], (NODES, D), 0.35, 2.09375, ((0, 32),)),
        "tile_dest": draw_tile_dest(jax.random.fold_in(arg_keys[8], 71), 0),
        "tile_source": draw_tile_source(jax.random.fold_in(arg_keys[8], 71), 0),
        "tile_count": draw_tile_count(jax.random.fold_in(arg_keys[8], 71), 0),
        "pattern_id": with_ends(jax.random.randint(arg_keys[4], (STOPS, FIBERS, STOPS, CAP), 0, BANK), jax.random.fold_in(arg_keys[4], 1), 0, BANK - 1).astype(jnp.int32),
        "pattern_bank": with_ends(jax.random.randint(arg_keys[5], (BANK, WORDS, TILE), -2147483648, 2147483647), jax.random.fold_in(arg_keys[5], 1), -2147483648, 2147483646).astype(jnp.int32),
        "negative_dest": with_ends(jax.random.randint(arg_keys[6], (STOPS, FIBERS, STOPS, NEG), 0, PT), jax.random.fold_in(arg_keys[6], 1), 0, PT - 1).astype(jnp.int32),
        "negative_source": with_ends(jax.random.randint(arg_keys[7], (STOPS, FIBERS, STOPS, NEG), 0, SUB), jax.random.fold_in(arg_keys[7], 1), 0, SUB - 1).astype(jnp.int32),
    }


def unpack_bits(packed_words):
    shifts = jnp.arange(32, dtype=jnp.int32)
    bit_values = jnp.right_shift(packed_words[:, :, None, :], shifts[None, None, :, None]) & 1
    return bit_values.reshape(packed_words.shape[0], packed_words.shape[1] * 32, packed_words.shape[2])

def reference(embedding, tile_dest, tile_source, tile_count, pattern_id, pattern_bank, negative_dest, negative_source):
    node_tiles = embedding.reshape(NODES // TILE, TILE, D)
    fibers = jnp.arange(FIBERS, dtype=jnp.int32)[:, None]
    slot_index = jnp.arange(CAP, dtype=jnp.int32)[None, :]

    def visit(flat_index, gradient_sum):
        block_index = flat_index // STOPS
        stop_index = flat_index % STOPS
        anchor = (block_index - stop_index) % STOPS
        live_slots = (slot_index < tile_count[block_index, :, stop_index][:, None]).astype(jnp.float32)
        live_slots = jnp.concatenate([live_slots, jnp.ones((FIBERS, NEG), jnp.float32)], axis=1).reshape(-1)
        dest_local = jnp.concatenate([tile_dest[block_index, :, stop_index], negative_dest[block_index, :, stop_index]], axis=1)
        source_local = jnp.concatenate([tile_source[block_index, :, stop_index], negative_source[block_index, :, stop_index]], axis=1)
        dest_ids = (block_index * PT + dest_local).reshape(-1).astype(jnp.int32)
        source_ids = (anchor * PT + fibers * SUB + source_local).reshape(-1).astype(jnp.int32)
        packed_words = pattern_bank[pattern_id[block_index, :, stop_index].reshape(-1)]
        mask_bits = unpack_bits(packed_words).astype(jnp.float32).reshape(FIBERS, CAP, TILE, TILE)
        mask_bits = jnp.concatenate([mask_bits, jnp.zeros((FIBERS, NEG, TILE, TILE), jnp.float32)], axis=1)
        mask_bits = mask_bits.reshape(FIBERS * (CAP + NEG), TILE, TILE)
        dest_rows = node_tiles[dest_ids].astype(jnp.float32)
        source_rows = node_tiles[source_ids].astype(jnp.float32)
        scores = jnp.einsum('gjd,gid->gji', source_rows, dest_rows, precision=lax.Precision.HIGHEST)
        residual = (live_slots[:, None, None] * (mask_bits - jax.nn.sigmoid(scores))).astype(jnp.bfloat16)
        residual = lax.optimization_barrier(residual).astype(jnp.float32)
        to_dest = jnp.einsum('gji,gjd->gid', residual, source_rows, precision=lax.Precision.HIGHEST)
        to_source = jnp.einsum('gji,gid->gjd', residual, dest_rows, precision=lax.Precision.HIGHEST)
        return gradient_sum.at[dest_ids].add(to_dest).at[source_ids].add(to_source)
    gradient_sum = lax.fori_loop(0, STOPS * STOPS, visit, jnp.zeros((NODES // TILE, TILE, D), jnp.float32))
    return (gradient_sum / jnp.sqrt(jnp.float32(TILE * STOPS))).reshape(NODES, D)
```

```python
import functools

import jax
import jax.numpy as jnp
from jax import lax
from jax.experimental import pallas as pl
from jax.experimental.pallas import tpu as pltpu
from jax.sharding import PartitionSpec as P

LANES = 128
UNROLL = 4
SRC_AT, FIBER_AT, MASK_AT = 6, 12, 19
COL_AT, WORK_MASK_AT = 8, 20


def bank_kernel(bank_ref, out_ref):
    patterns, words, tile = bank_ref.shape
    shift = 31 - lax.broadcasted_iota(jnp.int32, (32, tile), 0)
    row = lax.broadcasted_iota(jnp.int32, (16, tile), 0)
    lane = lax.broadcasted_iota(jnp.int32, (16, tile), 1)
    in_row = (lane // 32 == row % words) & ((lane % 32) // 16 == row // words)
    weight = jnp.where(in_row, jnp.left_shift(1, lane % 16), 0).astype(jnp.float32).astype(jnp.bfloat16)
    out_ref[patterns] = jnp.zeros((words, tile), jnp.int32)
    out_ref[2 * patterns + 1] = jnp.zeros((words, tile), jnp.int32)

    def turn(pattern, _):
        packed = bank_ref[pattern]
        rows = [
            jnp.where(jnp.left_shift(packed[w : w + 1, :], shift) < 0, 1.0, 0.0)
            for w in range(words)
        ]
        bits = jnp.concatenate(rows, axis=0).astype(jnp.bfloat16)
        halves = lax.dot_general(
            weight, bits, (((1,), (1,)), ((), ())), preferred_element_type=jnp.float32
        ).astype(jnp.int32)
        out_ref[pattern] = packed
        out_ref[patterns + 1 + pattern] = halves[:words] + jnp.left_shift(
            halves[words : 2 * words], 16
        )
        return 0

    lax.fori_loop(0, patterns, turn, 0, unroll=4)


def turned_bank(pattern_bank):
    patterns, words, tile = pattern_bank.shape
    return pl.pallas_call(
        bank_kernel,
        out_shape=jax.ShapeDtypeStruct((2 * patterns + 2, words, tile), jnp.int32),
        in_specs=[pl.BlockSpec(memory_space=pltpu.VMEM)],
        out_specs=pl.BlockSpec(memory_space=pltpu.VMEM),
        cost_estimate=pl.CostEstimate(flops=10**8, bytes_accessed=10**6, transcendentals=0),
        name="bank",
    )(pattern_bank)


def stage_kernel(columns, sub, blocks, first, patterns, *refs):
    shifts = sorted({dz for dz, _ in columns})
    flips = sorted({k for _, k in columns})
    refs = list(refs)
    place_ref = refs.pop(0)
    pair_refs = {k: refs.pop(0) for k in flips}
    ring_refs = {dz: refs.pop(0) for dz in shifts}
    column_refs = [refs.pop(0) for _ in columns]
    rows_ref = refs.pop(0)
    bank_ref = refs.pop(0)
    before_ref = None if first else refs.pop(0)
    acc_ref, held, work, sems = refs

    copies = [
        pltpu.make_async_copy(ref, held.at[pl.ds(at * sub, sub)], sems.at[at])
        for at, ref in enumerate(column_refs)
    ]
    for copy in copies:
        copy.start()
    if first:
        acc_ref[...] = jnp.zeros_like(acc_ref)
    else:
        acc_ref[...] = before_ref[...]

    block = place_ref[0]
    fiber = place_ref[1]
    partner = place_ref[2]

    def scan(line_at, owner, item_of, filled):
        def some(group, filled):
            for step in range(4):
                word = line_at(group * 4 + step)
                work[filled] = item_of(word)
                filled += (((word >> FIBER_AT) & 127) == owner).astype(jnp.int32)
            return filled

        return lax.fori_loop(0, (line_at(LANES - 1) + 3) >> 2, some, filled)

    filled = jnp.int32(0)
    for at, (dz, k) in enumerate(columns):
        there = lax.rem(block + (blocks - 2 * dz), blocks)
        for r, mine in enumerate((block, partner)):
            stop = lax.rem(mine - there + blocks, blocks)
            filled = scan(
                lambda j, k=k, r=r, stop=stop: pair_refs[k][r, stop, j],
                fiber,
                lambda word, r=r, at=at: ((word & 63) + r * sub)
                + ((((word >> SRC_AT) & 63) + at * sub) << COL_AT)
                + (((word >> MASK_AT) + patterns + 1) << WORK_MASK_AT),
                filled,
            )
            stop = lax.rem(there - mine + blocks, blocks)
            filled = scan(
                lambda j, dz=dz, stop=stop: ring_refs[dz][stop, j],
                fiber ^ k,
                lambda word, r=r, at=at: (((word >> SRC_AT) & 63) + r * sub)
                + (((word & 63) + at * sub) << COL_AT)
                + ((word >> MASK_AT) << WORK_MASK_AT),
                filled,
            )
    for step in range(UNROLL):
        work[filled + step] = 2 * sub + (patterns << WORK_MASK_AT)

    for copy in copies:
        copy.wait()

    words, tile = bank_ref.shape[1:]
    shift = 31 - lax.broadcasted_iota(jnp.int32, (32, tile), 0)

    def some_items(group, _):
        for step in range(UNROLL):
            item = work[group * UNROLL + step]
            own = item & 255
            other = held[(item >> COL_AT) & 4095]
            packed = bank_ref[item >> WORK_MASK_AT]
            half = lax.dot_general(
                rows_ref[own], other, (((1,), (1,)), ((), ())), preferred_element_type=jnp.float32
            )
            sign = jnp.concatenate(
                [
                    jnp.where(jnp.left_shift(packed[w : w + 1, :], shift) < 0, 1.0, -1.0)
                    for w in range(words)
                ],
                axis=0,
            )
            residual = (sign - jnp.tanh(half)).astype(jnp.bfloat16)
            acc_ref[own] += jnp.dot(residual, other, preferred_element_type=jnp.float32)
        return 0

    lax.fori_loop(0, lax.div(filled + (UNROLL - 1), UNROLL), some_items, 0)


def stage(columns, place, pair_tables, ring_tables, arrays, rows, bank, acc, sub, blocks):
    tiles, tile, width = rows.shape
    patterns = bank.shape[0] // 2 - 1
    shifts = sorted({dz for dz, _ in columns})
    flips = sorted({k for _, k in columns})
    first = acc is None
    most = len(columns) * 4 * LANES
    smem = pl.BlockSpec(memory_space=pltpu.SMEM)
    vmem = pl.BlockSpec(memory_space=pltpu.VMEM)
    operands = [place] + [pair_tables[k] for k in flips] + [ring_tables[dz] for dz in shifts]
    specs = [smem] * len(operands)
    operands += [a.reshape(sub, tile, width) for a in arrays]
    specs += [pl.BlockSpec(memory_space=pl.ANY)] * len(arrays)
    operands += [rows, bank]
    specs += [vmem, vmem]
    if not first:
        operands.append(acc)
        specs.append(vmem)
    pairs = 16 * len(columns)
    return pl.pallas_call(
        functools.partial(stage_kernel, columns, sub, blocks, first, patterns),
        out_shape=jax.ShapeDtypeStruct((tiles, tile, width), jnp.float32),
        in_specs=specs,
        out_specs=vmem,
        scratch_shapes=[
            pltpu.VMEM((len(columns) * sub, tile, width), jnp.bfloat16),
            pltpu.SMEM((most,), jnp.int32),
            pltpu.SemaphoreType.DMA((len(columns),)),
        ],
        input_output_aliases={} if first else {len(operands) - 1: 0},
        cost_estimate=pl.CostEstimate(
            flops=pairs * 4 * tile * tile * width, bytes_accessed=4 * 10**6, transcendentals=pairs * tile * tile
        ),
        name="stage",
    )(*operands)


def on_device(
    embedding, tile_dest, tile_source, tile_count, pattern_id, pattern_bank, negative_dest, negative_source
):
    local_rows, width = embedding.shape
    patterns, words, tile = pattern_bank.shape
    sub = local_rows // tile
    blocks = lax.axis_size("blk")
    fibers = lax.axis_size("fiber")
    ring = blocks // 2
    block = lax.axis_index("blk")
    fiber = lax.axis_index("fiber")

    def swap(value):
        return lax.ppermute(value, "blk", [(i, i ^ 1) for i in range(blocks)])

    def flip(value, k):
        return lax.ppermute(value, "fiber", [(i, i ^ k) for i in range(fibers)])

    def along(value, dz):
        return lax.ppermute(value, "blk", [(i, (i + 2 * dz) % blocks) for i in range(blocks)])

    dest = jnp.concatenate([negative_dest[0, 0], tile_dest[0, 0]], axis=1)
    source = jnp.concatenate([negative_source[0, 0], tile_source[0, 0]], axis=1)
    mask = jnp.concatenate([jnp.full_like(negative_dest[0, 0], patterns), pattern_id[0, 0]], axis=1)
    word = dest % sub + (source << SRC_AT) + ((dest // sub) << FIBER_AT) + (mask << MASK_AT)
    slots = word.shape[1]
    count = tile_count[0, 0][:, None] + negative_dest.shape[3]
    word = jnp.where(jnp.arange(slots, dtype=jnp.int32)[None, :] < count, word, 127 << FIBER_AT)
    word = jnp.pad(word, ((0, 0), (0, LANES - 1 - slots)), constant_values=127 << FIBER_AT)
    table = jnp.concatenate([word, count], axis=1)

    pair_tables = {0: jnp.stack([table, swap(table)])}
    for k in range(1, fibers):
        pair_tables[k] = flip(pair_tables[0], k)
    ring_tables = {0: table}
    for dz in range(1, ring):
        ring_tables[dz] = along(table, dz)
    place = jnp.stack([block, fiber, block ^ 1]).astype(jnp.int32)

    both = jnp.concatenate([embedding, swap(embedding), jnp.zeros((tile, width), embedding.dtype)])
    rows = (both * jnp.asarray(0.5, embedding.dtype)).reshape(2 * sub + 1, tile, width)
    bank = turned_bank(pattern_bank)

    half = local_rows // 2
    got = {(0, 0): embedding}
    bits = [1 << i for i in range(fibers.bit_length() - 1)]

    def spread(dz):
        for k in bits:
            got[dz, k] = flip(got[dz, 0], k)

    def across(dz):
        for k in range(1, fibers):
            if k in bits:
                continue
            low = k & -k
            high = 1 << (k.bit_length() - 1)
            got[dz, k] = jnp.concatenate(
                [flip(got[dz, k ^ low][:half], low), flip(got[dz, k ^ high][half:], high)]
            )

    spread(0)
    got[1, 0] = along(embedding, 1)
    got[ring - 1, 0] = along(embedding, ring - 1)
    across(0)
    order = [1, ring - 1]
    for step in range(2, ring // 2 + 1):
        got[step, 0] = along(got[step - 1, 0], 1)
        order.append(step)
        if step != ring - step:
            got[ring - step, 0] = along(got[ring - step + 1, 0], ring - 1)
            order.append(ring - step)
    for dz in order:
        spread(dz)
    diagonal = [k for k in range(1, fibers) if k not in bits]
    for k in diagonal:
        got[1, k] = along(got[0, k], 1)
        got[ring - 1, k] = along(got[0, k], ring - 1)
    for dz in order[2:]:
        across(dz)

    groups = [[(0, 0)], [(0, k) for k in bits], [(1, 0), (ring - 1, 0)]]
    groups.append([(0, k) for k in diagonal] + [(1, k) for k in bits])
    groups.append([(ring - 1, k) for k in bits] + [(dz, 0) for dz in order[2:]])
    groups.append([(1, k) for k in diagonal] + [(dz, k) for dz in order[2:] for k in bits])
    groups.append([(ring - 1, k) for k in diagonal] + [(dz, k) for dz in order[2:] for k in diagonal])
    acc = None
    for columns in groups:
        acc = stage(
            columns, place, pair_tables, ring_tables, [got[c] for c in columns], rows, bank, acc, sub, blocks
        )
    total = acc[:sub] + swap(acc[sub : 2 * sub])
    scale = jnp.float32(0.5) / jnp.sqrt(jnp.float32(tile * blocks))
    return total.reshape(local_rows, width) * scale


def solution(mesh):
    listed = P("blk", "fiber", None, None)
    in_specs = (
        P(("blk", "fiber"), None),
        listed,
        listed,
        P("blk", "fiber", None),
        listed,
        P(),
        listed,
        listed,
    )
    return jax.shard_map(
        on_device, mesh=mesh, in_specs=in_specs, out_specs=P(("blk", "fiber"), None), check_vma=False
    )
```

```python
import functools

import jax
import jax.numpy as jnp
from jax import lax
from jax.experimental import pallas as pl
from jax.experimental.pallas import tpu as pltpu
from jax.sharding import PartitionSpec as P

LANES = 128
UNROLL = 3
COL_AT, MASK_AT = 8, 20
HALF_AT, STARTS_AT = 32, 64


def bank_kernel(bank_ref, out_ref):
    patterns, words, tile = bank_ref.shape
    shift = 31 - lax.broadcasted_iota(jnp.int32, (32, tile), 0)
    row = lax.broadcasted_iota(jnp.int32, (16, tile), 0)
    lane = lax.broadcasted_iota(jnp.int32, (16, tile), 1)
    in_row = (lane // 32 == row % words) & ((lane % 32) // 16 == row // words)
    weight = jnp.where(in_row, jnp.left_shift(1, lane % 16), 0).astype(jnp.float32).astype(jnp.bfloat16)
    out_ref[patterns] = jnp.zeros((words, tile), jnp.int32)
    out_ref[2 * patterns + 1] = jnp.zeros((words, tile), jnp.int32)

    def turn(pattern, _):
        packed = bank_ref[pattern]
        rows = [
            jnp.where(jnp.left_shift(packed[w : w + 1, :], shift) < 0, 1.0, 0.0)
            for w in range(words)
        ]
        bits = jnp.concatenate(rows, axis=0).astype(jnp.bfloat16)
        halves = lax.dot_general(
            weight, bits, (((1,), (1,)), ((), ())), preferred_element_type=jnp.float32
        ).astype(jnp.int32)
        out_ref[pattern] = packed
        out_ref[patterns + 1 + pattern] = halves[:words] + jnp.left_shift(
            halves[words : 2 * words], 16
        )
        return 0

    lax.fori_loop(0, patterns, turn, 0, unroll=4)


def turned_bank(pattern_bank):
    patterns, words, tile = pattern_bank.shape
    return pl.pallas_call(
        bank_kernel,
        out_shape=jax.ShapeDtypeStruct((2 * patterns + 2, words, tile), jnp.int32),
        in_specs=[pl.BlockSpec(memory_space=pltpu.VMEM)],
        out_specs=pl.BlockSpec(memory_space=pltpu.VMEM),
        cost_estimate=pl.CostEstimate(flops=10**8, bytes_accessed=10**6, transcendentals=0),
        compiler_params=pltpu.CompilerParams(vmem_limit_bytes=4 * 2**20),
        name="bank",
    )(pattern_bank)


def stage_kernel(columns, sub, blocks, first, patterns, *refs):
    shifts = sorted({dz for dz, _ in columns})
    flips = sorted({k for _, k in columns})
    refs = list(refs)
    place_ref = refs.pop(0)
    home_ref = refs.pop(0)
    plane_ref = refs.pop(0) if flips != [0] else None
    ring_refs = {dz: refs.pop(0) for dz in shifts}
    column_refs = [refs.pop(0) for _ in columns]
    rows_ref = refs.pop(0)
    bank_ref = refs.pop(0)
    before_ref = None if first else refs.pop(0)
    acc_ref, held, scores, later_scores, residuals, later_residuals, work, waiting, sems = refs

    words, tile = bank_ref.shape[1:]
    copies = [
        pltpu.make_async_copy(ref.at[pl.ds(0, sub * tile)], held.at[pl.ds(at * sub * tile, sub * tile)], sems.at[at])
        for at, ref in enumerate(column_refs)
    ]
    for copy in copies:
        copy.start()
    if first:
        acc_ref[...] = jnp.zeros_like(acc_ref)
    else:
        acc_ref[...] = before_ref[...]
    empty = len(columns) * sub
    held[pl.ds(empty * tile, tile), :] = jnp.zeros((tile, held.shape[1]), held.dtype)
    nothing = (empty << COL_AT) + (patterns << MASK_AT)

    block = place_ref[0]
    fiber = place_ref[1]
    partner = place_ref[2]

    for own in range(2 * sub):
        waiting[own] = -1
    for step in range(4 * UNROLL):
        work[step] = 2 * sub + nothing

    def scan(line, at, owner, base, filled):
        def one(slot, filled):
            item = line[slot + at] + base
            own = item & 255
            earlier = waiting[own]
            work[filled] = earlier
            work[filled + 1] = item
            waiting[own] = jnp.where(earlier < 0, item, -1)
            return filled + jnp.where(earlier < 0, 0, 2)

        return lax.fori_loop(line[STARTS_AT + owner], line[STARTS_AT + 1 + owner], one, filled)

    filled = jnp.int32(4 * UNROLL)
    for at, (dz, k) in enumerate(columns):
        there = lax.rem(block + (blocks - 2 * dz), blocks)
        for r, mine in enumerate((block, partner)):
            stop = lax.rem(mine - there + blocks, blocks)
            base = r * sub + (at * sub << COL_AT) + (patterns + 1 << MASK_AT)
            lines = plane_ref.at[r, k - 1] if k else home_ref.at[r]
            filled = scan(lines.at[stop], 0, fiber, base, filled)
            stop = lax.rem(there - mine + blocks, blocks)
            base = r * sub + (at * sub << COL_AT)
            filled = scan(ring_refs[dz].at[stop], HALF_AT, fiber ^ k, base, filled)
    for own in range(2 * sub):
        earlier = waiting[own]
        work[filled] = earlier
        work[filled + 1] = own + nothing
        filled += jnp.where(earlier < 0, 0, 2)
    for step in range(10 * UNROLL):
        work[filled + step] = 2 * sub + nothing

    for copy in copies:
        copy.wait()

    shift = 31 - lax.broadcasted_iota(jnp.int32, (32, tile), 0)

    def pair_at(index):
        items = work[index], work[index + 1]
        others = [
            held[pl.ds(pl.multiple_of(((item >> COL_AT) & 4095) * tile, tile), tile), :] for item in items
        ]
        return items, jnp.concatenate(others, axis=0)

    def signs(item):
        packed = bank_ref[item >> MASK_AT]
        return jnp.concatenate(
            [
                jnp.where(jnp.left_shift(packed[w : w + 1, :], shift) < 0, 1.0, -1.0)
                for w in range(words)
            ],
            axis=0,
        )

    def one_group(group, scored, scoring, ready, readying):
        for step in range(UNROLL):
            items, others = pair_at(2 * (group * UNROLL + step))
            acc_ref[items[0] & 255] += jnp.dot(ready[step], others, preferred_element_type=jnp.float32)
        for step in range(UNROLL):
            index = 2 * ((group + 1) * UNROLL + step)
            sign = jnp.concatenate([signs(work[index]), signs(work[index + 1])], axis=1)
            readying[step] = (sign - jnp.tanh(scored[step])).astype(jnp.bfloat16)
        for step in range(UNROLL):
            items, others = pair_at(2 * ((group + 2) * UNROLL + step))
            scoring[step] = lax.dot_general(
                rows_ref[items[0] & 255],
                others,
                (((1,), (1,)), ((), ())),
                preferred_element_type=jnp.float32,
            )

    def two_groups(step, _):
        one_group(2 * step, later_scores, scores, residuals, later_residuals)
        one_group(2 * step + 1, scores, later_scores, later_residuals, residuals)
        return 0

    lax.fori_loop(0, lax.div(filled + (4 * UNROLL - 1), 4 * UNROLL), two_groups, 0)


def stage(columns, place, home, plane, rings, arrays, rows, bank, acc, sub, blocks):
    tiles, tile, width = rows.shape
    patterns = bank.shape[0] // 2 - 1
    shifts = sorted({dz for dz, _ in columns})
    first = acc is None
    most = len(columns) * 4 * 2 * HALF_AT + 4 * tiles + 16 * UNROLL
    smem = pl.BlockSpec(memory_space=pltpu.SMEM)
    vmem = pl.BlockSpec(memory_space=pltpu.VMEM)
    operands = [place, home]
    if any(k for _, k in columns):
        operands.append(plane)
    operands += [rings[dz] for dz in shifts]
    specs = [smem] * len(operands)
    operands += list(arrays)
    specs += [pl.BlockSpec(memory_space=pl.ANY)] * len(arrays)
    operands += [rows, bank]
    specs += [vmem, vmem]
    if not first:
        operands.append(acc)
        specs.append(vmem)
    return pl.pallas_call(
        functools.partial(stage_kernel, columns, sub, blocks, first, patterns),
        out_shape=jax.ShapeDtypeStruct((tiles, tile, width), jnp.float32),
        in_specs=specs,
        out_specs=vmem,
        scratch_shapes=[
            pltpu.VMEM(((len(columns) * sub + 1) * tile, width), jnp.bfloat16),
            pltpu.VMEM((UNROLL, tile, 2 * tile), jnp.float32),
            pltpu.VMEM((UNROLL, tile, 2 * tile), jnp.float32),
            pltpu.VMEM((UNROLL, tile, 2 * tile), jnp.bfloat16),
            pltpu.VMEM((UNROLL, tile, 2 * tile), jnp.bfloat16),
            pltpu.SMEM((most,), jnp.int32),
            pltpu.SMEM((tiles,), jnp.int32),
            pltpu.SemaphoreType.DMA((len(columns),)),
        ],
        input_output_aliases={} if first else {len(operands) - 1: 0},
        cost_estimate=pl.CostEstimate(
            flops=len(columns) * 10**9, bytes_accessed=10**6, transcendentals=10**5
        ),
        compiler_params=pltpu.CompilerParams(vmem_limit_bytes=24 * 2**20),
        name="stage",
    )(*operands)


def coded_table(dest, source, mask, count, sub, width):
    stops, slots = dest.shape
    at = jnp.arange(slots, dtype=jnp.int32)
    lane = jnp.arange(width, dtype=jnp.int32)[None, :, None]
    owner = jnp.where(at[None, :] < count[:, None], dest // sub, LANES)
    before = (owner[:, None, :] < owner[:, :, None]) | (
        (owner[:, None, :] == owner[:, :, None]) & (at[None, None, :] < at[None, :, None])
    )
    rank = jnp.sum(before.astype(jnp.int32), axis=2)[:, None, :]
    here = rank == lane % HALF_AT
    tile = (dest % sub)[:, None, :]
    start = (owner[:, None, :] < lane - STARTS_AT).astype(jnp.int32)
    swapped = (lane // HALF_AT + lane // LANES) % 2 == 1
    which = jnp.where(here, jnp.where(swapped, source[:, None, :], tile), 0)
    which = jnp.where(lane % LANES < STARTS_AT, which, jnp.where(lane < LANES, start, 0))
    masks = jnp.where(here & (lane < STARTS_AT), mask[:, None, :], 0)
    lines = jnp.concatenate([jnp.sum(which, axis=2), jnp.sum(masks, axis=2)], axis=0)
    return lines.astype(jnp.bfloat16)


def items_of(lines):
    lines = lines.astype(jnp.int32)
    stops = lines.shape[-2] // 2
    tiles, masks = lines[..., :stops, :], lines[..., stops:, :]
    return tiles[..., :LANES] + (tiles[..., LANES : 2 * LANES] << COL_AT) + (masks[..., :LANES] << MASK_AT)


def on_device(
    embedding, tile_dest, tile_source, tile_count, pattern_id, pattern_bank, negative_dest, negative_source
):
    local_rows, width = embedding.shape
    patterns, words, tile = pattern_bank.shape
    sub = local_rows // tile
    blocks = lax.axis_size("blk")
    fibers = lax.axis_size("fiber")
    ring = blocks // 2
    block = lax.axis_index("blk")
    fiber = lax.axis_index("fiber")

    def swap(value):
        return lax.ppermute(value, "blk", [(i, i ^ 1) for i in range(blocks)])

    def flip(value, k):
        return lax.ppermute(value, "fiber", [(i, i ^ k) for i in range(fibers)])

    def along(value, dz):
        return lax.ppermute(value, "blk", [(i, (i + 2 * dz) % blocks) for i in range(blocks)])

    dest = jnp.concatenate([negative_dest[0, 0], tile_dest[0, 0]], axis=1)
    source = jnp.concatenate([negative_source[0, 0], tile_source[0, 0]], axis=1)
    mask = jnp.concatenate([jnp.full_like(negative_dest[0, 0], patterns), pattern_id[0, 0]], axis=1)
    lines = coded_table(dest, source, mask, tile_count[0, 0] + negative_dest.shape[3], sub, width)
    parcel = jnp.concatenate([embedding, lines])
    place = jnp.stack([block, fiber, block ^ 1]).astype(jnp.int32)
    bank = turned_bank(pattern_bank)

    other = swap(parcel)
    got = {(0, 0): parcel}
    flips = range(1, fibers)
    for k in flips:
        got[0, k] = flip(parcel, k)
    got[1, 0] = along(parcel, 1)
    got[ring - 1, 0] = along(parcel, ring - 1)

    both = jnp.concatenate([embedding, other[:local_rows], jnp.zeros((tile, width), embedding.dtype)])
    rows = (both * jnp.asarray(0.5, embedding.dtype)).reshape(2 * sub + 1, tile, width)
    home = items_of(jnp.stack([lines, other[local_rows:]]))
    plane = jnp.stack([got[0, k][local_rows:] for k in flips])
    plane = items_of(jnp.stack([plane, swap(plane)]))
    rings = {0: home[0]}

    bits = [1 << i for i in range(fibers.bit_length() - 1)]
    rest = [k for k in flips if k not in bits]
    order = [1, ring - 1]
    for step in range(2, ring // 2 + 1):
        got[step, 0] = along(got[step - 1, 0], 1)
        order.append(step)
        if step != ring - step:
            got[ring - step, 0] = along(got[ring - step + 1, 0], ring - 1)
            order.append(ring - step)
    for dz in order:
        rings[dz] = items_of(got[dz, 0][local_rows:])
        for k in bits:
            got[dz, k] = flip(got[dz, 0], k)
    for dz in order:
        nearer = 1 if dz <= ring // 2 else ring - 1
        for k in rest:
            got[dz, k] = along(got[(dz - nearer) % ring, k], nearer)

    late = order[2:]
    groups = [[(0, 0)], [(0, k) for k in flips], [(dz, 0) for dz in order[:2]]]
    groups.append([(dz, k) for dz in order[:2] for k in bits])
    groups.append([(dz, k) for dz in order[:2] for k in rest] + [(dz, 0) for dz in late])
    groups.append([(dz, k) for dz in late for k in flips])
    acc = None
    for columns in groups:
        acc = stage(
            columns, place, home, plane, rings, [got[c] for c in columns], rows, bank, acc, sub, blocks
        )
    total = acc[:sub] + swap(acc[sub : 2 * sub])
    scale = jnp.float32(0.5) / jnp.sqrt(jnp.float32(tile * blocks))
    return total.reshape(local_rows, width) * scale


def solution(mesh):
    listed = P("blk", "fiber", None, None)
    in_specs = (
        P(("blk", "fiber"), None),
        listed,
        listed,
        P("blk", "fiber", None),
        listed,
        P(),
        listed,
        listed,
    )
    return jax.shard_map(
        on_device, mesh=mesh, in_specs=in_specs, out_specs=P(("blk", "fiber"), None), check_vma=False
    )
```

```python
import functools

import jax
import jax.numpy as jnp
from jax import lax
from jax.experimental import pallas as pl
from jax.experimental.pallas import tpu as pltpu
from jax.sharding import PartitionSpec as P


LANES = 128
UNROLL = 3
COL_AT, MASK_AT = 8, 20
HALF_AT, STARTS_AT = 32, 64


def bank_kernel(bank_ref, out_ref):
    patterns, words, tile = bank_ref.shape
    shift = 31 - lax.broadcasted_iota(jnp.int32, (32, tile), 0)
    row = lax.broadcasted_iota(jnp.int32, (16, tile), 0)
    lane = lax.broadcasted_iota(jnp.int32, (16, tile), 1)
    in_row = (lane // 32 == row % words) & ((lane % 32) // 16 == row // words)
    weight = jnp.where(in_row, jnp.left_shift(1, lane % 16), 0).astype(jnp.float32).astype(jnp.bfloat16)
    out_ref[patterns] = jnp.zeros((words, tile), jnp.int32)
    out_ref[2 * patterns + 1] = jnp.zeros((words, tile), jnp.int32)

    def turn(pattern, _):
        packed = bank_ref[pattern]
        rows = [
            jnp.where(jnp.left_shift(packed[w : w + 1, :], shift) < 0, 1.0, 0.0)
            for w in range(words)
        ]
        bits = jnp.concatenate(rows, axis=0).astype(jnp.bfloat16)
        halves = lax.dot_general(
            weight, bits, (((1,), (1,)), ((), ())), preferred_element_type=jnp.float32
        ).astype(jnp.int32)
        out_ref[pattern] = packed
        out_ref[patterns + 1 + pattern] = halves[:words] + jnp.left_shift(
            halves[words : 2 * words], 16
        )
        return 0

    lax.fori_loop(0, patterns, turn, 0, unroll=16)


def turned_bank(pattern_bank):
    patterns, words, tile = pattern_bank.shape
    return pl.pallas_call(
        bank_kernel,
        out_shape=jax.ShapeDtypeStruct((2 * patterns + 2, words, tile), jnp.int32),
        in_specs=[pl.BlockSpec(memory_space=pltpu.VMEM)],
        out_specs=pl.BlockSpec(memory_space=pltpu.VMEM),
        cost_estimate=pl.CostEstimate(flops=10**8, bytes_accessed=10**6, transcendentals=0),
        compiler_params=pltpu.CompilerParams(vmem_limit_bytes=4 * 2**20),
        name="bank",
    )(pattern_bank)


def stage_kernel(columns, sub, blocks, first, patterns, *refs):
    shifts = sorted({dz for dz, _ in columns})
    flips = sorted({k for _, k in columns})
    refs = list(refs)
    place_ref = refs.pop(0)
    plane_refs = {k: refs.pop(0) for k in flips}
    ring_refs = {dz: refs.pop(0) for dz in shifts}
    column_refs = [refs.pop(0) for _ in columns]
    rows_ref = refs.pop(0)
    bank_ref = refs.pop(0)
    before_ref = None if first else refs.pop(0)
    acc_ref, held, scores, later_scores, residuals, later_residuals, work, waiting, sems = refs

    words, tile = bank_ref.shape[1:]
    copies = [
        pltpu.make_async_copy(ref.at[pl.ds(0, sub * tile)], held.at[pl.ds(at * sub * tile, sub * tile)], sems.at[at])
        for at, ref in enumerate(column_refs)
    ]
    for copy in copies:
        copy.start()
    if first:
        acc_ref[...] = jnp.zeros_like(acc_ref)
    else:
        acc_ref[...] = before_ref[...]
    empty = len(columns) * sub
    held[pl.ds(empty * tile, tile), :] = jnp.zeros((tile, held.shape[1]), held.dtype)
    nothing = (empty << COL_AT) + (patterns << MASK_AT)

    block = place_ref[0]
    fiber = place_ref[1]
    partner = place_ref[2]

    for own in range(2 * sub):
        waiting[own] = -1
    for step in range(4 * UNROLL):
        work[step] = 2 * sub + nothing

    def scan(line, at, owner, base, filled):
        def one(slot, filled):
            item = line[slot + at] + base
            own = item & 255
            earlier = waiting[own]
            work[filled] = earlier
            work[filled + 1] = item
            waiting[own] = jnp.where(earlier < 0, item, -1)
            return filled + jnp.where(earlier < 0, 0, 2)

        return lax.fori_loop(line[STARTS_AT + owner], line[STARTS_AT + 1 + owner], one, filled)

    filled = jnp.int32(4 * UNROLL)
    for at, (dz, k) in enumerate(columns):
        there = lax.rem(block + (blocks - 2 * dz), blocks)
        for r, mine in enumerate((block, partner)):
            stop = lax.rem(mine - there + blocks, blocks)
            base = r * sub + (at * sub << COL_AT) + (patterns + 1 << MASK_AT)
            filled = scan(plane_refs[k].at[r, stop], 0, fiber, base, filled)
            stop = lax.rem(there - mine + blocks, blocks)
            base = r * sub + (at * sub << COL_AT)
            filled = scan(ring_refs[dz].at[stop], HALF_AT, fiber ^ k, base, filled)
    for own in range(2 * sub):
        earlier = waiting[own]
        work[filled] = earlier
        work[filled + 1] = own + nothing
        filled += jnp.where(earlier < 0, 0, 2)
    for step in range(10 * UNROLL):
        work[filled + step] = 2 * sub + nothing

    for copy in copies:
        copy.wait()

    shift = 31 - lax.broadcasted_iota(jnp.int32, (32, tile), 0)

    def pair_at(index):
        items = work[index], work[index + 1]
        others = [
            held[pl.ds(pl.multiple_of(((item >> COL_AT) & 4095) * tile, tile), tile), :] for item in items
        ]
        return items, jnp.concatenate(others, axis=0)

    def signs(item):
        packed = bank_ref[item >> MASK_AT]
        return jnp.concatenate(
            [
                jnp.where(jnp.left_shift(packed[w : w + 1, :], shift) < 0, 1.0, -1.0)
                for w in range(words)
            ],
            axis=0,
        )

    def one_group(group, scored, scoring, ready, readying):
        for step in range(UNROLL):
            items, others = pair_at(2 * (group * UNROLL + step))
            acc_ref[items[0] & 255] += jnp.dot(ready[step], others, preferred_element_type=jnp.float32)
        for step in range(UNROLL):
            index = 2 * ((group + 1) * UNROLL + step)
            sign = jnp.concatenate([signs(work[index]), signs(work[index + 1])], axis=1)
            readying[step] = (sign - jnp.tanh(scored[step])).astype(jnp.bfloat16)
        for step in range(UNROLL):
            items, others = pair_at(2 * ((group + 2) * UNROLL + step))
            scoring[step] = lax.dot_general(
                rows_ref[items[0] & 255],
                others,
                (((1,), (1,)), ((), ())),
                preferred_element_type=jnp.float32,
            )

    def two_groups(step, _):
        one_group(2 * step, later_scores, scores, residuals, later_residuals)
        one_group(2 * step + 1, scores, later_scores, later_residuals, residuals)
        return 0

    lax.fori_loop(0, lax.div(filled + (4 * UNROLL - 1), 4 * UNROLL), two_groups, 0)


def stage(columns, place, planes, rings, arrays, rows, bank, acc, sub, blocks):
    tiles, tile, width = rows.shape
    patterns = bank.shape[0] // 2 - 1
    shifts = sorted({dz for dz, _ in columns})
    first = acc is None
    most = len(columns) * 4 * 2 * HALF_AT + 4 * tiles + 16 * UNROLL
    smem = pl.BlockSpec(memory_space=pltpu.SMEM)
    vmem = pl.BlockSpec(memory_space=pltpu.VMEM)
    operands = [place] + [planes[k] for k in sorted({k for _, k in columns})] + [rings[dz] for dz in shifts]
    specs = [smem] * len(operands)
    operands += list(arrays)
    specs += [pl.BlockSpec(memory_space=pl.ANY)] * len(arrays)
    operands += [rows, bank]
    specs += [vmem, vmem]
    if not first:
        operands.append(acc)
        specs.append(vmem)
    return pl.pallas_call(
        functools.partial(stage_kernel, columns, sub, blocks, first, patterns),
        out_shape=jax.ShapeDtypeStruct((tiles, tile, width), jnp.float32),
        in_specs=specs,
        out_specs=vmem,
        scratch_shapes=[
            pltpu.VMEM(((len(columns) * sub + 1) * tile, width), jnp.bfloat16),
            pltpu.VMEM((UNROLL, tile, 2 * tile), jnp.float32),
            pltpu.VMEM((UNROLL, tile, 2 * tile), jnp.float32),
            pltpu.VMEM((UNROLL, tile, 2 * tile), jnp.bfloat16),
            pltpu.VMEM((UNROLL, tile, 2 * tile), jnp.bfloat16),
            pltpu.SMEM((most,), jnp.int32),
            pltpu.SMEM((tiles,), jnp.int32),
            pltpu.SemaphoreType.DMA((len(columns),)),
        ],
        input_output_aliases={} if first else {len(operands) - 1: 0},
        cost_estimate=pl.CostEstimate(
            flops=len(columns) * 10**9, bytes_accessed=10**6, transcendentals=10**5
        ),
        compiler_params=pltpu.CompilerParams(vmem_limit_bytes=24 * 2**20),
        name="stage",
    )(*operands)


def parcel_kernel(sub, patterns, *refs):
    operands, (out_ref, lines_ref), held, sems = refs[:7], refs[7:9], refs[9:15], refs[15]
    count_ref, dest_ref, source_ref, mask_ref, away_ref, from_ref = held
    local_rows, width = operands[6].shape
    targets = list(held) + [out_ref.at[pl.ds(0, local_rows)]]
    copies = [
        pltpu.make_async_copy(ref, to, sems.at[n]) for n, (ref, to) in enumerate(zip(operands, targets))
    ]
    for copy in copies:
        copy.start()
    for copy in copies[:6]:
        copy.wait()
    stops, slots = dest_ref.shape[2:]
    negatives = away_ref.shape[2]
    row = lax.broadcasted_iota(jnp.int32, (stops, slots), 0)
    listed = lax.broadcasted_iota(jnp.int32, (stops, slots), 1)
    negative = lax.broadcasted_iota(jnp.int32, (stops, negatives), 1)
    negative_row = lax.broadcasted_iota(jnp.int32, (stops, negatives), 0)
    count = jnp.zeros((stops, slots), jnp.int32)
    away = jnp.zeros((stops, negatives), jnp.int32)
    away_source = jnp.zeros((stops, negatives), jnp.int32)
    for stop in range(stops):
        count = jnp.where(row == stop, count_ref[0, 0, stop], count)
        for k in range(negatives):
            here = (negative_row == stop) & (negative == k)
            away = jnp.where(here, away_ref[0, 0, k, stop], away)
            away_source = jnp.where(here, from_ref[0, 0, k, stop], away_source)
    dest = dest_ref[0, 0]
    owner = jnp.where(listed < count, dest // sub, LANES)
    away_owner = away // sub
    rank = jnp.zeros((stops, slots), jnp.int32)
    away_rank = jnp.zeros((stops, negatives), jnp.int32)
    one = lambda test: jnp.where(test, 1, 0)
    for k in range(slots):
        this = owner[:, k : k + 1]
        rank += one((this < owner) | ((this == owner) & (k < listed)))
        away_rank += one(this <= away_owner)
    for k in range(negatives):
        this = away_owner[:, k : k + 1]
        away_rank += one((this < away_owner) | ((this == away_owner) & (k < negative)))
        rank += one(this < owner)

    lane = lax.broadcasted_iota(jnp.int32, (stops, width), 1)
    at = lane % HALF_AT
    swapped = (lane // HALF_AT + lane // LANES) % 2 == 1
    which = jnp.zeros((stops, width), jnp.int32)
    masks = jnp.full((stops, width), patterns, jnp.int32)
    starts = jnp.zeros((stops, width), jnp.int32)
    tile, away_tile = dest % sub, away % sub
    source = source_ref[0, 0]
    mask = mask_ref[0, 0]
    for k in range(slots):
        col = slice(k, k + 1)
        here = at == rank[:, col]
        which = jnp.where(here, jnp.where(swapped, source[:, col], tile[:, col]), which)
        masks = jnp.where(here, mask[:, col], masks)
        starts += one(owner[:, col] < lane - STARTS_AT)
    for k in range(negatives):
        col = slice(k, k + 1)
        here = at == away_rank[:, col]
        which = jnp.where(here, jnp.where(swapped, away_source[:, col], away_tile[:, col]), which)
        masks = jnp.where(here, patterns, masks)
        starts += one(away_owner[:, col] < lane - STARTS_AT)
    which = jnp.where(lane % LANES < STARTS_AT, which, jnp.where(lane < LANES, starts, 0))
    masks = jnp.where(lane < STARTS_AT, masks, 0)
    lines = jnp.concatenate([which, masks], axis=0).astype(jnp.float32).astype(out_ref.dtype)
    out_ref[pl.ds(local_rows, 2 * stops), :] = lines
    lines_ref[...] = lines
    copies[6].wait()


def parcel_of(embedding, tile_dest, tile_source, tile_count, pattern_id, negative_dest, negative_source, tile, patterns):
    local_rows, width = embedding.shape
    stops = tile_dest.shape[2]
    operands = [
        tile_count,
        tile_dest,
        tile_source,
        pattern_id,
        jnp.swapaxes(negative_dest, 2, 3),
        jnp.swapaxes(negative_source, 2, 3),
    ]
    spaces = [pltpu.SMEM] + [pltpu.VMEM] * 3 + [pltpu.SMEM] * 2
    return pl.pallas_call(
        functools.partial(parcel_kernel, local_rows // tile, patterns),
        out_shape=[
            jax.ShapeDtypeStruct((local_rows + 2 * stops, width), embedding.dtype),
            jax.ShapeDtypeStruct((2 * stops, width), embedding.dtype),
        ],
        in_specs=[pl.BlockSpec(memory_space=pl.ANY)] * 7,
        out_specs=[pl.BlockSpec(memory_space=pltpu.VMEM)] * 2,
        scratch_shapes=[space(value.shape, jnp.int32) for space, value in zip(spaces, operands)]
        + [pltpu.SemaphoreType.DMA((7,))],
        cost_estimate=pl.CostEstimate(flops=10**8, bytes_accessed=10**6, transcendentals=0),
        compiler_params=pltpu.CompilerParams(vmem_limit_bytes=60 * 2**20),
        name="parcel",
    )(*operands, embedding)


def items_of(lines):
    lines = lines.astype(jnp.int32)
    stops = lines.shape[-2] // 2
    tiles, masks = lines[..., :stops, :], lines[..., stops:, :]
    return tiles[..., :LANES] + (tiles[..., LANES : 2 * LANES] << COL_AT) + (masks[..., :LANES] << MASK_AT)


def on_device(
    embedding, tile_dest, tile_source, tile_count, pattern_id, pattern_bank, negative_dest, negative_source
):
    local_rows, width = embedding.shape
    patterns, _, tile = pattern_bank.shape
    sub = local_rows // tile
    blocks = lax.axis_size("blk")
    fibers = lax.axis_size("fiber")
    ring = blocks // 2
    block = lax.axis_index("blk")
    fiber = lax.axis_index("fiber")

    def swap(value):
        return lax.ppermute(value, "blk", [(i, i ^ 1) for i in range(blocks)])

    def flip(value, k):
        return lax.ppermute(value, "fiber", [(i, i ^ k) for i in range(fibers)])

    def along(value, dz):
        return lax.ppermute(value, "blk", [(i, (i + 2 * dz) % blocks) for i in range(blocks)])

    parcel, lines = parcel_of(
        embedding,
        tile_dest,
        tile_source,
        tile_count,
        pattern_id,
        negative_dest,
        negative_source,
        tile,
        patterns,
    )
    place = jnp.stack([block, fiber, block ^ 1]).astype(jnp.int32)
    bank = turned_bank(pattern_bank)

    other = swap(parcel)
    got = {(0, 0): parcel}
    flips = range(1, fibers)
    bits = [1 << i for i in range(fibers.bit_length() - 1)]
    rest = [k for k in flips if k not in bits]
    for k in flips:
        got[0, k] = flip(parcel, k)
    got[1, 0] = along(parcel, 1)
    got[ring - 1, 0] = along(parcel, ring - 1)

    both = jnp.concatenate([embedding, other[:local_rows], jnp.zeros((tile, width), embedding.dtype)])
    rows = (both * jnp.asarray(0.5, embedding.dtype)).reshape(2 * sub + 1, tile, width)
    home = items_of(jnp.stack([lines, other[local_rows:]]))
    planes = {}
    for some in (bits, rest):
        plane = jnp.stack([got[0, k][local_rows:] for k in some])
        plane = items_of(jnp.stack([plane, swap(plane)]))
        planes |= {k: plane[:, at] for at, k in enumerate(some)}
    planes[0] = home
    rings = {0: home[0]}

    order = [1, ring - 1]
    for step in range(2, ring // 2 + 1):
        got[step, 0] = along(got[step - 1, 0], 1)
        order.append(step)
        if step != ring - step:
            got[ring - step, 0] = along(got[ring - step + 1, 0], ring - 1)
            order.append(ring - step)
    late = order[2:]
    for dz in order:
        rings[dz] = items_of(got[dz, 0][local_rows:])
        for k in bits:
            got[dz, k] = flip(got[dz, 0], k)
    for place_in, dz in enumerate(order):
        for k in rest:
            if place_in < 2:
                got[dz, k] = along(got[0, k], dz)
            else:
                got[dz, k] = flip(got[dz, 0], k)

    groups = [[(0, 0)], [(0, k) for k in bits], [(dz, 0) for dz in order[:2]]]
    groups.append([(0, k) for k in rest] + [(order[0], k) for k in bits])
    groups.append([(order[1], k) for k in bits] + [(dz, 0) for dz in late])
    groups.append([(dz, k) for dz in order[:2] for k in rest] + [(dz, k) for dz in late for k in flips])
    acc = None
    for columns in groups:
        acc = stage(columns, place, planes, rings, [got[c] for c in columns], rows, bank, acc, sub, blocks)
    total = acc[:sub] + swap(acc[sub : 2 * sub])
    scale = jnp.float32(0.5) / jnp.sqrt(jnp.float32(tile * blocks))
    return total.reshape(local_rows, width) * scale


def solution(mesh):
    listed = P("blk", "fiber", None, None)
    in_specs = (
        P(("blk", "fiber"), None),
        listed,
        listed,
        P("blk", "fiber", None),
        listed,
        P(),
        listed,
        listed,
    )

    return jax.shard_map(on_device, mesh=mesh, in_specs=in_specs, out_specs=P(("blk", "fiber"), None), check_vma=False)
```

```python
import functools

import jax
import jax.numpy as jnp
from jax import lax
from jax.experimental import pallas as pl
from jax.experimental.pallas import tpu as pltpu
from jax.sharding import PartitionSpec as P


LANES = 128
UNROLL = 3
COL_AT, MASK_AT = 8, 20
HALF_AT, STARTS_AT = 32, 64


def bank_kernel(bank_ref, out_ref):
    patterns, words, tile = bank_ref.shape
    shift = 31 - lax.broadcasted_iota(jnp.int32, (32, tile), 0)
    row = lax.broadcasted_iota(jnp.int32, (16, tile), 0)
    lane = lax.broadcasted_iota(jnp.int32, (16, tile), 1)
    in_row = (lane // 32 == row % words) & ((lane % 32) // 16 == row // words)
    weight = jnp.where(in_row, jnp.left_shift(1, lane % 16), 0).astype(jnp.float32).astype(jnp.bfloat16)
    out_ref[patterns] = jnp.zeros((words, tile), jnp.int32)
    out_ref[2 * patterns + 1] = jnp.zeros((words, tile), jnp.int32)

    def turn(pattern, _):
        packed = bank_ref[pattern]
        rows = [
            jnp.where(jnp.left_shift(packed[w : w + 1, :], shift) < 0, 1.0, 0.0)
            for w in range(words)
        ]
        bits = jnp.concatenate(rows, axis=0).astype(jnp.bfloat16)
        halves = lax.dot_general(
            weight, bits, (((1,), (1,)), ((), ())), preferred_element_type=jnp.float32
        ).astype(jnp.int32)
        out_ref[pattern] = packed
        out_ref[patterns + 1 + pattern] = halves[:words] + jnp.left_shift(
            halves[words : 2 * words], 16
        )
        return 0

    lax.fori_loop(0, patterns, turn, 0, unroll=16)


def turned_bank(pattern_bank):
    patterns, words, tile = pattern_bank.shape
    return pl.pallas_call(
        bank_kernel,
        out_shape=jax.ShapeDtypeStruct((2 * patterns + 2, words, tile), jnp.int32),
        in_specs=[pl.BlockSpec(memory_space=pltpu.VMEM)],
        out_specs=pl.BlockSpec(memory_space=pltpu.VMEM),
        cost_estimate=pl.CostEstimate(flops=10**8, bytes_accessed=10**6, transcendentals=0),
        compiler_params=pltpu.CompilerParams(vmem_limit_bytes=4 * 2**20),
        name="bank",
    )(pattern_bank)


def stage_kernel(columns, sub, blocks, first, patterns, *refs):
    shifts = sorted({dz for dz, _ in columns})
    flips = sorted({k for _, k in columns})
    refs = list(refs)
    place_ref = refs.pop(0)
    plane_refs = {k: refs.pop(0) for k in flips}
    ring_refs = {dz: refs.pop(0) for dz in shifts}
    column_refs = [refs.pop(0) for _ in columns]
    rows_ref = refs.pop(0)
    bank_ref = refs.pop(0)
    before_ref = None if first else refs.pop(0)
    acc_ref, held, scores, later_scores, residuals, later_residuals, work, waiting, sems = refs

    words, tile = bank_ref.shape[1:]
    copies = [
        pltpu.make_async_copy(ref.at[pl.ds(0, sub * tile)], held.at[pl.ds(at * sub * tile, sub * tile)], sems.at[at])
        for at, ref in enumerate(column_refs)
    ]
    for copy in copies:
        copy.start()
    if first:
        acc_ref[...] = jnp.zeros_like(acc_ref)
    else:
        acc_ref[...] = before_ref[...]
    empty = len(columns) * sub
    held[pl.ds(empty * tile, tile), :] = jnp.zeros((tile, held.shape[1]), held.dtype)
    nothing = (empty << COL_AT) + (patterns << MASK_AT)

    block = place_ref[0]
    fiber = place_ref[1]
    partner = place_ref[2]

    for own in range(2 * sub):
        waiting[own] = -1
    for step in range(4 * UNROLL):
        work[step] = 2 * sub + nothing

    def scan(line, at, owner, base, filled):
        def one(slot, filled):
            item = line[slot + at] + base
            own = item & 255
            earlier = waiting[own]
            work[filled] = earlier
            work[filled + 1] = item
            waiting[own] = jnp.where(earlier < 0, item, -1)
            return filled + jnp.where(earlier < 0, 0, 2)

        return lax.fori_loop(line[STARTS_AT + owner], line[STARTS_AT + 1 + owner], one, filled)

    filled = jnp.int32(4 * UNROLL)
    for at, (dz, k) in enumerate(columns):
        there = lax.rem(block + (blocks - 2 * dz), blocks)
        for r, mine in enumerate((block, partner)):
            stop = lax.rem(mine - there + blocks, blocks)
            base = r * sub + (at * sub << COL_AT) + (patterns + 1 << MASK_AT)
            filled = scan(plane_refs[k].at[r, stop], 0, fiber, base, filled)
            stop = lax.rem(there - mine + blocks, blocks)
            base = r * sub + (at * sub << COL_AT)
            filled = scan(ring_refs[dz].at[stop], HALF_AT, fiber ^ k, base, filled)
    for own in range(2 * sub):
        earlier = waiting[own]
        work[filled] = earlier
        work[filled + 1] = own + nothing
        filled += jnp.where(earlier < 0, 0, 2)
    for step in range(10 * UNROLL):
        work[filled + step] = 2 * sub + nothing

    for copy in copies:
        copy.wait()

    shift = 31 - lax.broadcasted_iota(jnp.int32, (32, tile), 0)

    def pair_at(index):
        items = work[index], work[index + 1]
        others = [
            held[pl.ds(pl.multiple_of(((item >> COL_AT) & 4095) * tile, tile), tile), :] for item in items
        ]
        return items, jnp.concatenate(others, axis=0)

    def signs(item):
        packed = bank_ref[item >> MASK_AT]
        return jnp.concatenate(
            [
                jnp.where(jnp.left_shift(packed[w : w + 1, :], shift) < 0, 1.0, -1.0)
                for w in range(words)
            ],
            axis=0,
        )

    def one_group(group, scored, scoring, ready, readying):
        for step in range(UNROLL):
            items, others = pair_at(2 * (group * UNROLL + step))
            acc_ref[items[0] & 255] += jnp.dot(ready[step], others, preferred_element_type=jnp.float32)
        for step in range(UNROLL):
            index = 2 * ((group + 1) * UNROLL + step)
            sign = jnp.concatenate([signs(work[index]), signs(work[index + 1])], axis=1)
            readying[step] = (sign - jnp.tanh(scored[step])).astype(jnp.bfloat16)
        for step in range(UNROLL):
            items, others = pair_at(2 * ((group + 2) * UNROLL + step))
            scoring[step] = lax.dot_general(
                rows_ref[items[0] & 255],
                others,
                (((1,), (1,)), ((), ())),
                preferred_element_type=jnp.float32,
            )

    def two_groups(step, _):
        one_group(2 * step, later_scores, scores, residuals, later_residuals)
        one_group(2 * step + 1, scores, later_scores, later_residuals, residuals)
        return 0

    lax.fori_loop(0, lax.div(filled + (4 * UNROLL - 1), 4 * UNROLL), two_groups, 0)


def stage(columns, place, planes, rings, arrays, rows, bank, acc, sub, blocks):
    tiles, tile, width = rows.shape
    patterns = bank.shape[0] // 2 - 1
    shifts = sorted({dz for dz, _ in columns})
    first = acc is None
    most = len(columns) * 4 * 2 * HALF_AT + 4 * tiles + 16 * UNROLL
    smem = pl.BlockSpec(memory_space=pltpu.SMEM)
    vmem = pl.BlockSpec(memory_space=pltpu.VMEM)
    operands = [place] + [planes[k] for k in sorted({k for _, k in columns})] + [rings[dz] for dz in shifts]
    specs = [smem] * len(operands)
    operands += list(arrays)
    specs += [pl.BlockSpec(memory_space=pl.ANY)] * len(arrays)
    operands += [rows, bank]
    specs += [vmem, vmem]
    if not first:
        operands.append(acc)
        specs.append(vmem)
    return pl.pallas_call(
        functools.partial(stage_kernel, columns, sub, blocks, first, patterns),
        out_shape=jax.ShapeDtypeStruct((tiles, tile, width), jnp.float32),
        in_specs=specs,
        out_specs=vmem,
        scratch_shapes=[
            pltpu.VMEM(((len(columns) * sub + 1) * tile, width), jnp.bfloat16),
            pltpu.VMEM((UNROLL, tile, 2 * tile), jnp.float32),
            pltpu.VMEM((UNROLL, tile, 2 * tile), jnp.float32),
            pltpu.VMEM((UNROLL, tile, 2 * tile), jnp.bfloat16),
            pltpu.VMEM((UNROLL, tile, 2 * tile), jnp.bfloat16),
            pltpu.SMEM((most,), jnp.int32),
            pltpu.SMEM((tiles,), jnp.int32),
            pltpu.SemaphoreType.DMA((len(columns),)),
        ],
        input_output_aliases={} if first else {len(operands) - 1: 0},
        cost_estimate=pl.CostEstimate(
            flops=len(columns) * 10**9, bytes_accessed=10**6, transcendentals=10**5
        ),
        compiler_params=pltpu.CompilerParams(vmem_limit_bytes=24 * 2**20),
        name="stage",
    )(*operands)


def parcel_kernel(sub, patterns, *refs):
    operands, (out_ref, lines_ref, bank_ref), held, sems = refs[:8], refs[8:11], refs[11:17], refs[17]
    count_ref, dest_ref, source_ref, mask_ref, away_ref, from_ref = held
    local_rows, width = operands[6].shape
    targets = list(held) + [out_ref.at[pl.ds(0, local_rows)], bank_ref]
    copies = [
        pltpu.make_async_copy(ref, to, sems.at[n]) for n, (ref, to) in enumerate(zip(operands, targets))
    ]
    for copy in copies:
        copy.start()
    for copy in copies[:6]:
        copy.wait()
    stops, slots = dest_ref.shape[2:]
    negatives = away_ref.shape[2]
    row = lax.broadcasted_iota(jnp.int32, (stops, slots), 0)
    listed = lax.broadcasted_iota(jnp.int32, (stops, slots), 1)
    negative = lax.broadcasted_iota(jnp.int32, (stops, negatives), 1)
    negative_row = lax.broadcasted_iota(jnp.int32, (stops, negatives), 0)
    count = jnp.zeros((stops, slots), jnp.int32)
    away = jnp.zeros((stops, negatives), jnp.int32)
    away_source = jnp.zeros((stops, negatives), jnp.int32)
    for stop in range(stops):
        count = jnp.where(row == stop, count_ref[0, 0, stop], count)
        for k in range(negatives):
            here = (negative_row == stop) & (negative == k)
            away = jnp.where(here, away_ref[0, 0, k, stop], away)
            away_source = jnp.where(here, from_ref[0, 0, k, stop], away_source)
    dest = dest_ref[0, 0]
    owner = jnp.where(listed < count, dest // sub, LANES)
    away_owner = away // sub
    rank = jnp.zeros((stops, slots), jnp.int32)
    away_rank = jnp.zeros((stops, negatives), jnp.int32)
    one = lambda test: jnp.where(test, 1, 0)
    for k in range(slots):
        this = owner[:, k : k + 1]
        rank += one((this < owner) | ((this == owner) & (k < listed)))
        away_rank += one(this <= away_owner)
    for k in range(negatives):
        this = away_owner[:, k : k + 1]
        away_rank += one((this < away_owner) | ((this == away_owner) & (k < negative)))
        rank += one(this < owner)

    lane = lax.broadcasted_iota(jnp.int32, (stops, width), 1)
    at = lane % HALF_AT
    swapped = (lane // HALF_AT + lane // LANES) % 2 == 1
    which = jnp.zeros((stops, width), jnp.int32)
    masks = jnp.full((stops, width), patterns, jnp.int32)
    starts = jnp.zeros((stops, width), jnp.int32)
    tile, away_tile = dest % sub, away % sub
    source = source_ref[0, 0]
    mask = mask_ref[0, 0]
    for k in range(slots):
        col = slice(k, k + 1)
        here = at == rank[:, col]
        which = jnp.where(here, jnp.where(swapped, source[:, col], tile[:, col]), which)
        masks = jnp.where(here, mask[:, col], masks)
        starts += one(owner[:, col] < lane - STARTS_AT)
    for k in range(negatives):
        col = slice(k, k + 1)
        here = at == away_rank[:, col]
        which = jnp.where(here, jnp.where(swapped, away_source[:, col], away_tile[:, col]), which)
        masks = jnp.where(here, patterns, masks)
        starts += one(away_owner[:, col] < lane - STARTS_AT)
    which = jnp.where(lane % LANES < STARTS_AT, which, jnp.where(lane < LANES, starts, 0))
    masks = jnp.where(lane < STARTS_AT, masks, 0)
    lines = jnp.concatenate([which, masks], axis=0).astype(jnp.float32).astype(out_ref.dtype)
    out_ref[pl.ds(local_rows, 2 * stops), :] = lines
    lines_ref[...] = lines
    for copy in copies[6:]:
        copy.wait()


def parcel_of(embedding, tile_dest, tile_source, tile_count, pattern_id, negative_dest, negative_source, pattern_bank):
    local_rows, width = embedding.shape
    patterns, _, tile = pattern_bank.shape
    stops = tile_dest.shape[2]
    operands = [
        tile_count,
        tile_dest,
        tile_source,
        pattern_id,
        jnp.swapaxes(negative_dest, 2, 3),
        jnp.swapaxes(negative_source, 2, 3),
    ]
    spaces = [pltpu.SMEM] + [pltpu.VMEM] * 3 + [pltpu.SMEM] * 2
    return pl.pallas_call(
        functools.partial(parcel_kernel, local_rows // tile, patterns),
        out_shape=[
            jax.ShapeDtypeStruct((local_rows + 2 * stops, width), embedding.dtype),
            jax.ShapeDtypeStruct((2 * stops, width), embedding.dtype),
            jax.ShapeDtypeStruct(pattern_bank.shape, jnp.int32),
        ],
        in_specs=[pl.BlockSpec(memory_space=pl.ANY)] * 8,
        out_specs=[pl.BlockSpec(memory_space=pltpu.VMEM)] * 3,
        scratch_shapes=[space(value.shape, jnp.int32) for space, value in zip(spaces, operands)]
        + [pltpu.SemaphoreType.DMA((8,))],
        cost_estimate=pl.CostEstimate(flops=10**8, bytes_accessed=10**6, transcendentals=0),
        compiler_params=pltpu.CompilerParams(vmem_limit_bytes=60 * 2**20),
        name="parcel",
    )(*operands, embedding, pattern_bank)


def items_of(lines):
    lines = lines.astype(jnp.int32)
    stops = lines.shape[-2] // 2
    tiles, masks = lines[..., :stops, :], lines[..., stops:, :]
    return tiles[..., :LANES] + (tiles[..., LANES : 2 * LANES] << COL_AT) + (masks[..., :LANES] << MASK_AT)


def on_device(
    embedding, tile_dest, tile_source, tile_count, pattern_id, pattern_bank, negative_dest, negative_source
):
    local_rows, width = embedding.shape
    _, _, tile = pattern_bank.shape
    sub = local_rows // tile
    blocks = lax.axis_size("blk")
    fibers = lax.axis_size("fiber")
    ring = blocks // 2
    block = lax.axis_index("blk")
    fiber = lax.axis_index("fiber")

    def swap(value):
        return lax.ppermute(value, "blk", [(i, i ^ 1) for i in range(blocks)])

    def flip(value, k):
        return lax.ppermute(value, "fiber", [(i, i ^ k) for i in range(fibers)])

    def along(value, dz):
        return lax.ppermute(value, "blk", [(i, (i + 2 * dz) % blocks) for i in range(blocks)])

    parcel, lines, pattern_bank = parcel_of(
        embedding,
        tile_dest,
        tile_source,
        tile_count,
        pattern_id,
        negative_dest,
        negative_source,
        pattern_bank,
    )
    place = jnp.stack([block, fiber, block ^ 1]).astype(jnp.int32)
    bank = turned_bank(pattern_bank)

    other = swap(parcel)
    got = {(0, 0): parcel}
    flips = range(1, fibers)
    bits = [1 << i for i in range(fibers.bit_length() - 1)]
    rest = [k for k in flips if k not in bits]
    for k in flips:
        got[0, k] = flip(parcel, k)
    got[1, 0] = along(parcel, 1)
    got[ring - 1, 0] = along(parcel, ring - 1)

    both = jnp.concatenate([embedding, other[:local_rows], jnp.zeros((tile, width), embedding.dtype)])
    rows = (both * jnp.asarray(0.5, embedding.dtype)).reshape(2 * sub + 1, tile, width)
    home = items_of(jnp.stack([lines, other[local_rows:]]))
    planes = {}
    for some in (bits, rest):
        plane = jnp.stack([got[0, k][local_rows:] for k in some])
        plane = items_of(jnp.stack([plane, swap(plane)]))
        planes |= {k: plane[:, at] for at, k in enumerate(some)}
    planes[0] = home
    rings = {0: home[0]}

    order = [1, ring - 1]
    for step in range(2, ring // 2 + 1):
        got[step, 0] = along(got[step - 1, 0], 1)
        order.append(step)
        if step != ring - step:
            got[ring - step, 0] = along(got[ring - step + 1, 0], ring - 1)
            order.append(ring - step)
    late = order[2:]
    for dz in order:
        rings[dz] = items_of(got[dz, 0][local_rows:])
        for k in bits:
            got[dz, k] = flip(got[dz, 0], k)
    for place_in, dz in enumerate(order):
        for k in rest:
            if place_in < 2:
                got[dz, k] = along(got[0, k], dz)
            else:
                got[dz, k] = flip(got[dz, 0], k)

    groups = [[(0, 0)], [(0, k) for k in bits]]
    groups.append([(0, k) for k in rest] + [(dz, k) for dz in order[:2] for k in [0] + bits] + [(dz, 0) for dz in late])
    groups.append([(dz, k) for dz in order[:2] for k in rest] + [(dz, k) for dz in late for k in flips])
    acc = None
    for columns in groups:
        acc = stage(columns, place, planes, rings, [got[c] for c in columns], rows, bank, acc, sub, blocks)
    total = acc[:sub] + swap(acc[sub : 2 * sub])
    scale = jnp.float32(0.5) / jnp.sqrt(jnp.float32(tile * blocks))
    return total.reshape(local_rows, width) * scale


def solution(mesh):
    listed = P("blk", "fiber", None, None)
    in_specs = (
        P(("blk", "fiber"), None),
        listed,
        listed,
        P("blk", "fiber", None),
        listed,
        P(),
        listed,
        listed,
    )

    return jax.shard_map(on_device, mesh=mesh, in_specs=in_specs, out_specs=P(("blk", "fiber"), None), check_vma=False)
```
